32 devices in a mesh: blk: 8 (over z, y), tp: 4 (over x, core).
Axes of the slice: x: 2, y: 2, z: 4, core: 2. Of those that a mesh axis runs over, the one named last changes fastest.
Arguments:
- kv_keys: bfloat16 [32, 2048, 512], P('blk', None, 'tp'), may hold values from -6 to 6
- kv_values: bfloat16 [32, 2048, 512], P('blk', None, 'tp'), may hold values from -6 to 6
- queries: bfloat16 [32, 128, 3584], P('blk', None, 'tp'), may hold values from -170 to 170, as said below
- hidden: bfloat16 [32, 128, 3584], P('blk', None, 'tp'), may hold values from -2 to 2
- out_weight: bfloat16 [3584, 3584], P('tp'), may hold values from -0.09375 to 0.09375
- block_live: int32 [32], P('blk'), may hold values from 1 to 128
- node_tiles: int32 [32, 128], P('blk'), may hold values from 1 to 16
- left_count: int32 [8], P('blk'), may hold values from 1 to 2, as said below
- right_count: int32 [8], P('blk'), may hold values from 1 to 2, as said below
Outputs:
- balanced: bfloat16 [64, 128, 3584], P('blk', None, 'tp')
The draws below stay inside these ranges and needn't reach their ends.
Inputs may be any that keep to these rules, and one draw needn't show every extreme that they name: `queries`: queries of the nodes. `left_count`: at most 2; some index reaches 2 in every draw. `right_count`: at most 2; some index reaches 2 in every draw.
All inputs are finite; a program needn't handle non-finite values.
Results may differ from the reference program's by a relative error of at most 0.0047.
Values may be sent and summed in bfloat16 or wider, within the bound.
No kernel may reach another device: no remote copies, remote signals or barrier semaphores. Data moves between devices by JAX's collectives and lax.ppermute only.
A program may use at most 192 MiB of HBM per device.

```python
import jax
import jax.numpy as jnp
from jax import lax

D = 3584
QH = 28
KVH = 4
HD = 128
BT = 2048
TILE = 128
BLK_DEV = 4
S_MAX = 2
NPB = 128
TILES = 16
SLOTS = 8
BLOCKS = 32
N_BLK = 8


def pair_draw(key):
    base = jax.random.fold_in(key, 101)
    key_part = jnp.clip(jax.random.normal(jax.random.fold_in(base, 1), (BLOCKS, BT, KVH, HD), jnp.float32), -6.0, 6.0)
    query_part = jnp.clip(2.0 * jax.random.normal(jax.random.fold_in(base, 2), (BLOCKS, NPB, QH, HD), jnp.float32), -12.0, 12.0)
    return (key_part.reshape(BLOCKS, BT, KVH * HD), query_part.reshape(BLOCKS, NPB, QH * HD))


def draw_kv_keys(key, part):
    return pair_draw(key)[0].astype(jnp.bfloat16)


def draw_queries(key, part):
    return pair_draw(key)[1].astype(jnp.bfloat16)


def shift_draw(key):
    cycle_size = BLOCKS // BLK_DEV
    drawn = jax.random.randint(jax.random.fold_in(key, 1), (cycle_size,), 1, S_MAX + 1)
    chosen = jax.random.randint(jax.random.fold_in(key, 2), (), 0, cycle_size)
    return jnp.where(jnp.arange(cycle_size) == chosen, S_MAX, drawn).astype(jnp.int32)


def draw_left_count(key, part):
    return shift_draw(jax.random.fold_in(key, 201))


def draw_right_count(key, part):
    return shift_draw(jax.random.fold_in(key, 202))


def place_ends(values, key, low, top_value):
    extent = values.shape
    index_at = [jax.random.randint(jax.random.fold_in(key, axis), (), 0, extent[axis]) for axis in range(len(extent))]
    values = values.at[tuple(index_at)].set(low)
    longest = extent.index(max(extent))
    index_at[longest] = (index_at[longest] + 1) % extent[longest]
    return values.at[tuple(index_at)].set(top_value)


def block_levels(stream_key, shape, shards, smallest, top_value):
    def one(axis_at, blocks):
        draws = jax.random.uniform(jax.random.fold_in(jax.random.fold_in(stream_key, 6), axis_at), (blocks,), jnp.float32, smallest / len(shards), top_value / len(shards))
        return jnp.repeat(jnp.exp(draws), shape[axis_at] // blocks).reshape((-1,) + (1,) * (len(shape) - axis_at - 1))

    loudness = one(*shards[0])
    for cut in shards[1:]:
        loudness = loudness * one(*cut)
    return loudness


def centred(stream_key, shape, deviation, most, shards=(), kind=jnp.bfloat16):
    entries = jax.random.normal(stream_key, shape, jnp.float32) * deviation
    if len(shards) > 0:
        entries = block_levels(stream_key, shape, shards, -0.22, 0.18) * entries
    return jnp.clip(entries, min=-most, max=most).astype(kind)


def setup_inputs(seed: int = 0) -> dict:
    keys = jax.random.split(jax.random.key(seed), 10)
    return {
        "kv_keys": draw_kv_keys(jax.random.fold_in(keys[9], 71), 0),
        "kv_values": centred(keys[1], (BLOCKS, BT, KVH * HD), 1.0, 6.0, ((0, 8), (2, 4))),
        "queries": draw_queries(jax.random.fold_in(keys[9], 71), 0),
        "hidden": centred(keys[3], (BLOCKS, NPB, D), 0.3, 2.0, ((0, 8), (2, 4))),
        "out_weight": centred(keys[4], (QH * HD, D), (QH * HD) ** -0.5, 0.09375, ((0, 4),)),
        "block_live": place_ends(jax.random.randint(keys[5], (BLOCKS,), 1, NPB + 1), jax.random.fold_in(keys[5], 1), 1, NPB).astype(jnp.int32),
        "node_tiles": place_ends(jax.random.randint(keys[6], (BLOCKS, NPB), 1, TILES + 1), jax.random.fold_in(keys[6], 1), 1, TILES).astype(jnp.int32),
        "left_count": draw_left_count(jax.random.fold_in(keys[9], 71), 0),
        "right_count": draw_right_count(jax.random.fold_in(keys[9], 71), 0),
    }


def attend(query_rows, key_rows, value_rows, tiles):
    batch_size, node_count, row_width = query_rows.shape
    head_size = key_rows.shape[2]
    group_size = row_width // head_size
    flat_rows = query_rows.reshape(batch_size, node_count * group_size, head_size).astype(jnp.float32)
    scores = jnp.einsum('srd,spd->srp', flat_rows, key_rows.astype(jnp.float32)) * (head_size ** -0.5)
    reach = jnp.repeat(tiles, group_size, axis=1) * TILE
    places = lax.broadcasted_iota(jnp.int32, (1, 1, key_rows.shape[1]), 2)
    inside = places < reach[:, :, None]
    scores = jnp.where(inside, scores, jnp.float32(-1e30))
    row_max = jnp.max(scores, axis=-1, keepdims=True)
    weights_exp = jnp.where(inside, jnp.exp(scores - row_max), jnp.float32(0.0))
    weights = (weights_exp / jnp.sum(weights_exp, axis=-1, keepdims=True)).astype(jnp.bfloat16)
    mixed = jnp.einsum('srp,spd->srd', weights.astype(jnp.float32), value_rows.astype(jnp.float32))
    return mixed.astype(jnp.bfloat16).reshape(batch_size, node_count, row_width)


def reference(kv_keys, kv_values, queries, hidden, out_weight, block_live, node_tiles, left_count, right_count):
    group_size = QH // KVH

    def one_block(block_items):
        key_block, value_block, query_block, tile_block = block_items
        key_heads = key_block.reshape(BT, KVH, HD).transpose(1, 0, 2)
        value_heads = value_block.reshape(BT, KVH, HD).transpose(1, 0, 2)
        query_heads = query_block.reshape(NPB, KVH, group_size * HD).transpose(1, 0, 2)
        tile_heads = jnp.broadcast_to(tile_block[None, :], (KVH, NPB))
        result = attend(query_heads, key_heads, value_heads, tile_heads)
        return result.transpose(1, 0, 2).reshape(NPB, QH * HD)

    attn = lax.map(one_block, (kv_keys, kv_values, queries, node_tiles))
    projected = jnp.dot(attn.reshape(BLOCKS * NPB, QH * HD), out_weight, preferred_element_type=jnp.float32)
    node_out = hidden.astype(jnp.float32) + projected.reshape(BLOCKS, NPB, D)
    node_live = jnp.arange(NPB, dtype=jnp.int32)[None, :] < block_live[:, None]
    node_out = jnp.where(node_live[:, :, None], node_out, jnp.float32(0.0))
    device = jnp.arange(N_BLK, dtype=jnp.int32)[:, None]
    slot_index = jnp.arange(SLOTS, dtype=jnp.int32)[None, :]
    previous = (device - 1) % N_BLK
    following = (device + 1) % N_BLK
    from_prev = slot_index < S_MAX
    from_next = slot_index >= S_MAX + BLK_DEV
    source_dev = jnp.where(from_prev, previous, jnp.where(from_next, following, device))
    source_blk = jnp.where(from_prev, BLK_DEV - S_MAX + slot_index, jnp.where(from_next, slot_index - S_MAX - BLK_DEV, slot_index - S_MAX))
    own_usable = (source_blk >= left_count[device]) & (source_blk < BLK_DEV - right_count[device])
    usable = jnp.where(from_prev, S_MAX - slot_index <= right_count[previous], jnp.where(from_next, source_blk < left_count[following], own_usable))
    source_index = (source_dev * BLK_DEV + source_blk).reshape(-1).astype(jnp.int32)
    gathered = node_out[source_index]
    return jnp.where(usable.reshape(-1)[:, None, None], gathered, jnp.float32(0.0)).astype(jnp.bfloat16)
```

```python
import functools

import jax
import jax.numpy as jnp
from jax import lax
from jax.experimental import pallas as pl
from jax.experimental.pallas import tpu as pltpu
from jax.sharding import PartitionSpec as P

TILE = 128
S_MAX = 2
GROUP = 32
SEG = 512
LOG2E = 1.4426950408889634
MASKED = -1e30


def block_kernel(
    live_ref, shard_ref, q_ref, k_ref, v_ref, tiles_ref, w_hbm,
    send_ref, keep_ref,
    w_ref, kx_ref, vx_ref, qx_ref, s_ref, mx_ref, acc_ref, attn_ref, w_sem,
):
    block = shard_ref[4]
    w_copy = pltpu.make_async_copy(w_hbm, w_ref, w_sem)
    w_copy.start()
    nodes, width = q_ref.shape[1], q_ref.shape[2]
    hd = k_ref.shape[2]
    heads = width // hd
    places = k_ref.shape[1]
    shard_cols = send_ref.shape[2]
    scale = jnp.float32(hd**-0.5 * LOG2E)
    live = live_ref[block]

    kx_ref[:, :hd] = k_ref[0]
    tile_of = lax.broadcasted_iota(jnp.int32, (places, hd), 0) // TILE
    lane_of = lax.broadcasted_iota(jnp.int32, (places, hd), 1)
    kx_ref[:, hd:] = jnp.where(tile_of == lane_of, 1.0, 0.0).astype(jnp.bfloat16)
    vx_ref[:, :hd] = v_ref[0]
    vx_ref[:, hd:] = jnp.ones((places, hd), jnp.bfloat16)

    sub = lax.broadcasted_iota(jnp.int32, (nodes, nodes), 0)
    lane = lax.broadcasted_iota(jnp.int32, (nodes, nodes), 1)
    tiles_row = jnp.broadcast_to(tiles_ref[pl.ds(block, 1), :], (nodes, nodes))
    reach_row = jnp.where(lane < live, tiles_row, 0)
    key_row = (reach_row * nodes + (nodes - 1 - lane)).astype(jnp.float32)
    key_col = key_row.T
    above = jnp.where(key_col > key_row, 1.0, 0.0)
    rank_row = jnp.sum(above, axis=0, keepdims=True)
    below = jnp.where(key_row > key_col, 1.0, 0.0)
    rank_col = jnp.sum(below, axis=1, keepdims=True)
    to_sorted = rank_row == sub.astype(jnp.float32)
    to_nodes = jnp.where(rank_col == lane.astype(jnp.float32), 1.0, 0.0).astype(jnp.bfloat16)
    reach_sorted = jnp.sum(
        jnp.where(to_sorted, reach_row.astype(jnp.float32), 0.0), axis=1, keepdims=True
    )
    to_sorted = jnp.where(to_sorted, 1.0, 0.0).astype(jnp.bfloat16)
    q_sorted = jnp.dot(to_sorted, q_ref[0], preferred_element_type=jnp.float32).astype(jnp.bfloat16)
    seen = jnp.maximum(reach_sorted, 1.0)
    bias = jnp.where(lax.broadcasted_iota(jnp.int32, (nodes, hd), 1).astype(jnp.float32) < seen, 0.0, MASKED)
    bias = jnp.where(lax.broadcasted_iota(jnp.int32, (nodes, hd), 1) < places // TILE, bias, 0.0)
    bias = bias.astype(jnp.bfloat16)
    rows = heads * GROUP
    for g in range(nodes // GROUP):
        for h in range(heads):
            at = slice(g * rows + h * GROUP, g * rows + (h + 1) * GROUP)
            qx_ref[at, :hd] = q_sorted[g * GROUP : (g + 1) * GROUP, h * hd : (h + 1) * hd]
            qx_ref[at, hd:] = bias[g * GROUP : (g + 1) * GROUP]

    for g in range(nodes // GROUP):
        longest = jnp.max(reach_sorted[g * GROUP : (g + 1) * GROUP]).astype(jnp.int32)
        segs = (longest * TILE + SEG - 1) // SEG

        @pl.when(segs == 0)
        def _():
            attn_ref[g * GROUP : (g + 1) * GROUP, :] = jnp.zeros((GROUP, width), jnp.bfloat16)

        @pl.when(segs > 0)
        def _():
            mx_ref[...] = jnp.full(mx_ref.shape, MASKED, jnp.float32)
            acc_ref[...] = jnp.zeros_like(acc_ref)
            at = slice(g * rows, (g + 1) * rows)

            @pl.loop(0, segs)
            def _(i):
                places_at = pl.ds(pl.multiple_of(i * SEG, SEG), SEG)
                s = lax.dot_general(
                    qx_ref[at, :], kx_ref[places_at, :], (((1,), (1,)), ((), ())),
                    preferred_element_type=jnp.float32,
                )
                s_ref[:, places_at] = s
                m = s[:, :hd]
                for t in range(1, SEG // hd):
                    m = jnp.maximum(m, s[:, t * hd : (t + 1) * hd])
                mx_ref[...] = jnp.maximum(mx_ref[...], m)

            top = jnp.max(mx_ref[...], axis=1, keepdims=True)

            @pl.loop(0, segs)
            def _(i):
                places_at = pl.ds(pl.multiple_of(i * SEG, SEG), SEG)
                p = jnp.exp2((s_ref[:, places_at] - top) * scale).astype(jnp.bfloat16)
                acc_ref[...] += jnp.dot(p, vx_ref[places_at, :], preferred_element_type=jnp.float32)

            mixed = (acc_ref[:, :hd] / acc_ref[:, hd:]).astype(jnp.bfloat16)
            for h in range(heads):
                attn_ref[g * GROUP : (g + 1) * GROUP, h * hd : (h + 1) * hd] = mixed[
                    h * GROUP : (h + 1) * GROUP
                ]

    attn = jnp.dot(to_nodes, attn_ref[...], preferred_element_type=jnp.float32).astype(jnp.bfloat16)
    w_copy.wait()
    for s in range(4):
        cols = pl.ds(pl.multiple_of(shard_ref[s] * shard_cols, 128), shard_cols)
        part = jnp.dot(attn, w_ref[:, cols], preferred_element_type=jnp.float32).astype(jnp.bfloat16)
        if s < 2:
            send_ref[s] = part
        else:
            keep_ref[s - 2] = part


def block_partials(j, q, k, v, tiles, live, w, shards):
    blocks, nodes, width = q.shape
    places, hd = k.shape[1], k.shape[2]
    heads = width // hd
    rows = heads * GROUP
    cols = w.shape[1] // 4
    info = jnp.concatenate([shards, jnp.full((1,), j, jnp.int32)])
    out = jax.ShapeDtypeStruct((2, nodes, cols), jnp.bfloat16)
    grid_spec = pltpu.PrefetchScalarGridSpec(
        num_scalar_prefetch=2,
        grid=(1,),
        in_specs=[
            pl.BlockSpec((1, nodes, width), lambda i, *_: (j, 0, 0)),
            pl.BlockSpec((1, places, hd), lambda i, *_: (j, 0, 0)),
            pl.BlockSpec((1, places, hd), lambda i, *_: (j, 0, 0)),
            pl.BlockSpec((blocks, nodes), lambda i, *_: (0, 0)),
            pl.BlockSpec(memory_space=pl.ANY),
        ],
        out_specs=[
            pl.BlockSpec((2, nodes, cols), lambda i, *_: (0, 0, 0)),
            pl.BlockSpec((2, nodes, cols), lambda i, *_: (0, 0, 0)),
        ],
        scratch_shapes=[
            pltpu.VMEM(w.shape, jnp.bfloat16),
            pltpu.VMEM((places, 2 * hd), jnp.bfloat16),
            pltpu.VMEM((places, 2 * hd), jnp.bfloat16),
            pltpu.VMEM((heads * nodes, 2 * hd), jnp.bfloat16),
            pltpu.VMEM((rows, places), jnp.float32),
            pltpu.VMEM((rows, hd), jnp.float32),
            pltpu.VMEM((rows, 2 * hd), jnp.float32),
            pltpu.VMEM((nodes, width), jnp.bfloat16),
            pltpu.SemaphoreType.DMA,
        ],
    )
    return pl.pallas_call(
        block_kernel,
        grid_spec=grid_spec,
        out_shape=(out, out),
        compiler_params=pltpu.CompilerParams(vmem_limit_bytes=32 << 20),
        cost_estimate=pl.CostEstimate(
            flops=2 * nodes * width * (2 * places + w.shape[1]),
            bytes_accessed=w.size * 2 + 4 * places * hd,
            transcendentals=nodes * heads * places,
        ),
    )(live, info, q, k, v, tiles, w)


def on_device(
    kv_keys, kv_values, queries, hidden, out_weight, block_live, node_tiles, left_count, right_count
):
    blocks, nodes, _ = queries.shape
    tp = lax.axis_size("tp")
    ring = lax.axis_size("blk")
    me = lax.axis_index("tp")
    mine, mate = me, me ^ 1
    shards = jnp.stack([mate, mate ^ 2, mine, mine ^ 2]).astype(jnp.int32)
    to_mate = [(i, i ^ 1) for i in range(tp)]
    to_across = [(i, i ^ 2) for i in range(tp)]
    to_next = [(i, (i + 1) % ring) for i in range(ring)]
    to_prev = [(i, (i - 1) % ring) for i in range(ring)]
    left, right = left_count[0], right_count[0]
    own = [None] * blocks
    from_next = [None] * S_MAX
    from_prev = [None] * S_MAX
    zero = jnp.zeros((), jnp.bfloat16)
    for j in range(blocks):
        send, keep = block_partials(
            j, queries, kv_keys, kv_values, node_tiles, block_live, out_weight, shards
        )
        got = lax.ppermute(send, "tp", to_mate)
        across = (keep[1].astype(jnp.float32) + got[1].astype(jnp.float32)).astype(jnp.bfloat16)
        other = lax.ppermute(across, "tp", to_across)
        total = (
            keep[0].astype(jnp.float32)
            + got[0].astype(jnp.float32)
            + other.astype(jnp.float32)
            + hidden[j].astype(jnp.float32)
        )
        alive = jnp.arange(nodes, dtype=jnp.int32)[:, None] < block_live[j]
        result = jnp.where(alive, total, 0.0).astype(jnp.bfloat16)
        stays = (left <= j) & (j < blocks - right)
        own[j] = jnp.where(stays, result, zero)
        if j < S_MAX:
            from_next[j] = lax.ppermute(jnp.where(j < left, result, zero), "blk", to_prev)
        if j >= blocks - S_MAX:
            goes = blocks - j <= right
            from_prev[j - blocks + S_MAX] = lax.ppermute(
                jnp.where(goes, result, zero), "blk", to_next
            )
    return jnp.stack(from_prev + own + from_next)


def solution(mesh):
    return jax.shard_map(
        on_device,
        mesh=mesh,
        in_specs=(
            P("blk", None, "tp"),
            P("blk", None, "tp"),
            P("blk", None, "tp"),
            P("blk", None, "tp"),
            P("tp", None),
            P("blk"),
            P("blk", None),
            P("blk"),
            P("blk"),
        ),
        out_specs=P("blk", None, "tp"),
        check_vma=False,
    )
```

```python
import functools

import jax
import jax.numpy as jnp
from jax import lax
from jax.experimental import pallas as pl
from jax.experimental.pallas import tpu as pltpu
from jax.sharding import PartitionSpec as P


TILE = 128
S_MAX = 2
GROUP = 64
SEG = 512
LOG2E = 1.4426950408889634
MASKED = -1e30
VMEM_LIMIT = 60 << 20
CHUNKS = ((0, 2), (2, 2))


def group_softmax(n, qg, kx_ref, vx_ref, b, scale, hd):
    tops, outs = [], []
    for i in range(n):
        at = slice(i * SEG, (i + 1) * SEG)
        s = lax.dot_general(
            qg, kx_ref[b, at, :], (((1,), (1,)), ((), ())), preferred_element_type=jnp.float32
        )
        top = jnp.max(s, axis=1, keepdims=True)
        p = jnp.exp2((s - top) * scale).astype(jnp.bfloat16)
        tops.append(top)
        outs.append(jnp.dot(p, vx_ref[b, at, :], preferred_element_type=jnp.float32))
    if n == 1:
        acc = outs[0]
    else:
        top = functools.reduce(jnp.maximum, tops)
        acc = sum(o * jnp.exp2((t - top) * scale) for o, t in zip(outs, tops))
    return (acc[:, :hd] / acc[:, hd:]).astype(jnp.bfloat16)


def blocks_kernel(
    first, count, live_ref, q_hbm, k_hbm, v_hbm, hidden_hbm, tiles_hbm, w_hbm, order_hbm, *refs
):
    send_hbm, keep_hbm, mine_hbm = refs[:count], refs[count : 2 * count], refs[2 * count : 3 * count]
    (
        tiles_ref, hidden_ref, mine_ref, q_ref, w_ref, kx_ref, vx_ref, qx_ref, attn_ref, perm_ref,
        part_ref, segs_ref, sems,
    ) = refs[3 * count :]
    _, nodes, width = q_ref.shape
    places, hd = kx_ref.shape[1], kx_ref.shape[2] // 2
    heads = width // hd
    groups = nodes // GROUP
    rows = heads * GROUP
    shard_cols = part_ref.shape[2]
    scale = jnp.float32(hd**-0.5 * LOG2E)
    me = lax.axis_index("tp")
    x, core = me // 2, me % 2
    shards = [2 * x + 1 - core, 2 * (1 - x) + 1 - core, 2 * (1 - x) + core, me]

    tiles_copy = pltpu.make_async_copy(tiles_hbm, tiles_ref, sems.at[3, 0])
    q_copies, k_copies, v_copies = [], [], []
    for b in range(count):
        q_copies.append(pltpu.make_async_copy(q_hbm.at[first + b], q_ref.at[b], sems.at[0, b]))
        k_copies.append(
            pltpu.make_async_copy(k_hbm.at[first + b], kx_ref.at[b, :, pl.ds(0, hd)], sems.at[1, b])
        )
        v_copies.append(
            pltpu.make_async_copy(v_hbm.at[first + b], vx_ref.at[b, :, pl.ds(0, hd)], sems.at[2, b])
        )
    hidden_copy = pltpu.make_async_copy(hidden_hbm.at[pl.ds(first, count)], hidden_ref, sems.at[3, 1])
    mine_copies = [
        pltpu.make_async_copy(mine_ref.at[b], mine_hbm[b], sems.at[6, b]) for b in range(count)
    ]
    w_copies, out_copies = [], []
    for s in range(4):
        cols = pl.ds(pl.multiple_of(shards[s] * shard_cols, 128), shard_cols)
        into = w_ref.at[s // 2, :, pl.ds(s % 2 * shard_cols, shard_cols)]
        w_copies.append(pltpu.make_async_copy(w_hbm.at[:, cols], into, sems.at[4, s]))
        if s < 3:
            out_copies.append([
                pltpu.make_async_copy(
                    part_ref.at[s, pl.ds(b * nodes, nodes)],
                    send_hbm[b].at[s] if s < 2 else keep_hbm[b],
                    sems.at[7 + s, b],
                )
                for b in range(count)
            ])
    tiles_copy.start()
    for b in range(count):
        q_copies[b].start()
    for b in range(count):
        k_copies[b].start()
        v_copies[b].start()

    tile_of = lax.broadcasted_iota(jnp.int32, (places, hd), 0) // TILE
    lane_of = lax.broadcasted_iota(jnp.int32, (places, hd), 1)
    marks = jnp.where(tile_of == lane_of, 1.0, 0.0).astype(jnp.bfloat16)
    for b in range(count):
        kx_ref[b, :, hd:] = marks
        vx_ref[b, :, hd:] = jnp.ones((places, hd), jnp.bfloat16)
    attn_ref[...] = jnp.zeros_like(attn_ref)

    sub = lax.broadcasted_iota(jnp.int32, (nodes, nodes), 0)
    lane = lax.broadcasted_iota(jnp.int32, (nodes, nodes), 1)
    sub_f, lane_f = sub.astype(jnp.float32), lane.astype(jnp.float32)
    tiles_copy.wait()
    for b in range(count):
        live = live_ref[first + b]
        tiles_row = jnp.broadcast_to(tiles_ref[first + b : first + b + 1, :], (nodes, nodes))
        reach_row = jnp.where(lane < live, tiles_row, 0)
        key_row = (reach_row * nodes + (nodes - 1 - lane)).astype(jnp.float32)
        key_col = key_row.T
        rank_row = jnp.sum(jnp.where(key_col > key_row, 1.0, 0.0), axis=0, keepdims=True)
        rank_col = jnp.sum(jnp.where(key_row > key_col, 1.0, 0.0), axis=1, keepdims=True)
        alive = (rank_col == lane_f) & (sub < live)
        perm_ref[b] = jnp.where(alive, 1.0, 0.0).astype(jnp.bfloat16)
        to_sorted = rank_row == sub_f
        reach = jnp.sum(
            jnp.where(to_sorted, reach_row.astype(jnp.float32), 0.0), axis=1, keepdims=True
        )
        for g in range(groups):
            longest = jnp.max(reach[g * GROUP : (g + 1) * GROUP]).astype(jnp.int32)
            segs_ref[b * groups + g] = (longest * TILE + SEG - 1) // SEG
        hidden_from = (lane_f >= jnp.maximum(reach, 1.0)) & (lane < places // TILE)
        bias = jnp.where(hidden_from, MASKED, 0.0)[:, :hd].astype(jnp.bfloat16)
        q_copies[b].wait()
        q_sorted = jnp.dot(
            jnp.where(to_sorted, 1.0, 0.0).astype(jnp.bfloat16), q_ref[b],
            preferred_element_type=jnp.float32,
        ).astype(jnp.bfloat16)
        for g in range(groups):
            for h in range(heads):
                at = slice((b * groups + g) * rows + h * GROUP, (b * groups + g) * rows + (h + 1) * GROUP)
                qx_ref[at, :hd] = q_sorted[g * GROUP : (g + 1) * GROUP, h * hd : (h + 1) * hd]
                qx_ref[at, hd:] = bias[g * GROUP : (g + 1) * GROUP]

    for b in range(count):
        k_copies[b].wait()
        v_copies[b].wait()
        if b == 0:
            for s in range(4):
                w_copies[s].start()
            hidden_copy.start()

        @pl.loop(0, (live_ref[first + b] + GROUP - 1) // GROUP)
        def _(g):
            at = pl.ds(pl.multiple_of((b * groups + g) * rows, GROUP), rows)
            out_at = pl.ds(pl.multiple_of(b * nodes + g * GROUP, GROUP), GROUP)
            segs = segs_ref[b * groups + g]

            def attend(n):
                mixed = group_softmax(n, qx_ref[at, :], kx_ref, vx_ref, b, scale, hd)
                for h in range(heads):
                    attn_ref[out_at, h * hd : (h + 1) * hd] = mixed[h * GROUP : (h + 1) * GROUP]

            def pick(low, high):
                if low == high:
                    attend(low)
                else:
                    half = (low + high) // 2
                    pl.when(segs <= half)(functools.partial(pick, low, half))
                    pl.when(segs > half)(functools.partial(pick, half + 1, high))

            pick(1, places // SEG)

    for b in range(count):
        at = slice(b * nodes, (b + 1) * nodes)
        attn_ref[at, :] = jnp.dot(
            perm_ref[b], attn_ref[at, :], preferred_element_type=jnp.float32
        ).astype(jnp.bfloat16)
    w_copies[0].wait()
    w_copies[1].wait()
    part = jnp.dot(attn_ref[...], w_ref[0], preferred_element_type=jnp.float32)
    for s in range(2):
        part_ref[s] = part[:, s * shard_cols : (s + 1) * shard_cols].astype(jnp.bfloat16)
        for copy in out_copies[s]:
            copy.start()
    w_copies[2].wait()
    w_copies[3].wait()
    hidden_copy.wait()
    part = jnp.dot(attn_ref[...], w_ref[1], preferred_element_type=jnp.float32)
    part_ref[2] = part[:, :shard_cols].astype(jnp.bfloat16)
    for copy in out_copies[2]:
        copy.start()
    row = lax.broadcasted_iota(jnp.int32, (nodes, shard_cols), 0)
    for b in range(count):
        own = part[b * nodes : (b + 1) * nodes, shard_cols:]
        mine_ref[b] = jnp.where(
            row < live_ref[first + b], own + hidden_ref[b].astype(jnp.float32), 0.0
        )
        mine_copies[b].start()
    for copy in out_copies[0] + out_copies[1] + out_copies[2] + mine_copies:
        copy.wait()


def block_partials(first, count, q, k, v, hidden, tiles, live, w, order):
    _, nodes, width = q.shape
    places, hd = k.shape[1], k.shape[2]
    heads = width // hd
    cols = w.shape[1] // 4
    bf16, f32 = jnp.bfloat16, jnp.float32
    outs = (
        [jax.ShapeDtypeStruct((2, nodes, cols), bf16)] * count
        + [jax.ShapeDtypeStruct((nodes, cols), bf16)] * count
        + [jax.ShapeDtypeStruct((nodes, cols), f32)] * count
    )
    anywhere = pl.BlockSpec(memory_space=pl.ANY)
    grid_spec = pltpu.PrefetchScalarGridSpec(
        num_scalar_prefetch=1,
        grid=(1,),
        in_specs=[anywhere] * 7,
        out_specs=[anywhere] * len(outs),
        scratch_shapes=[
            pltpu.VMEM(tiles.shape, jnp.int32),
            pltpu.VMEM((count, nodes, cols), jnp.bfloat16),
            pltpu.VMEM((count, nodes, cols), jnp.float32),
            pltpu.VMEM((count, nodes, width), jnp.bfloat16),
            pltpu.VMEM((2, width, 2 * cols), jnp.bfloat16),
            pltpu.VMEM((count, places, 2 * hd), jnp.bfloat16),
            pltpu.VMEM((count, places, 2 * hd), jnp.bfloat16),
            pltpu.VMEM((count * heads * nodes, 2 * hd), jnp.bfloat16),
            pltpu.VMEM((count * nodes, width), jnp.bfloat16),
            pltpu.VMEM((count, nodes, nodes), jnp.bfloat16),
            pltpu.VMEM((3, count * nodes, cols), jnp.bfloat16),
            pltpu.SMEM((count * (nodes // GROUP),), jnp.int32),
            pltpu.SemaphoreType.DMA((10, max(4, count))),
        ],
    )
    return pl.pallas_call(
        functools.partial(blocks_kernel, first, count),
        grid_spec=grid_spec,
        out_shape=outs,
        compiler_params=pltpu.CompilerParams(vmem_limit_bytes=VMEM_LIMIT),
        cost_estimate=pl.CostEstimate(
            flops=2 * count * nodes * width * (2 * places + w.shape[1]),
            bytes_accessed=w.size * 2 + count * 4 * places * hd,
            transcendentals=count * nodes * heads * places,
        ),
    )(live, q, k, v, hidden, tiles, w, order)


def on_device(
    kv_keys, kv_values, queries, hidden, out_weight, block_live, node_tiles, left_count, right_count
):
    blocks, _, _ = queries.shape
    tp = lax.axis_size("tp")
    ring = lax.axis_size("blk")
    to_mate = [(i, i ^ 1) for i in range(tp)]
    to_across = [(i, i ^ 2) for i in range(tp)]
    to_next = [(i, (i + 1) % ring) for i in range(ring)]
    to_prev = [(i, (i - 1) % ring) for i in range(ring)]
    left, right = left_count[0], right_count[0]
    from_prev, own, from_next = [None] * S_MAX, [None] * blocks, [None] * S_MAX
    bf16, wide = jnp.bfloat16, jnp.float32
    zero = jnp.zeros((), bf16)
    sums = {}
    order = node_tiles
    for first, count in CHUNKS:
        outs = block_partials(
            first, count, queries, kv_keys, kv_values, hidden, node_tiles, block_live,
            out_weight, order,
        )
        for b in range(count):
            j = first + b
            send, keep, mine = outs[b], outs[count + b], outs[2 * count + b]
            got = lax.ppermute(send, "tp", to_mate)
            across = (keep.astype(wide) + got[1].astype(wide)).astype(bf16)
            other = lax.ppermute(across, "tp", to_across)
            sums[j] = (mine, got[0], other)
            order = across
    for j in range(blocks):
        mine, mates, other = sums[j]
        result = (mine + mates.astype(wide) + other.astype(wide)).astype(bf16)
        own[j] = jnp.zeros_like(result)
        if 0 < j < blocks - 1:
            own[j] = jnp.where((left <= j) & (j < blocks - right), result, zero)
        if j < S_MAX:
            sent = result if j == 0 else jnp.where(j < left, result, zero)
            from_next[j] = lax.ppermute(sent, "blk", to_prev)
        if j >= blocks - S_MAX:
            sent = result if j == blocks - 1 else jnp.where(blocks - j <= right, result, zero)
            from_prev[j - blocks + S_MAX] = lax.ppermute(sent, "blk", to_next)
    return jnp.stack(from_prev + own + from_next)


def solution(mesh):
    return jax.shard_map(
        on_device,
        mesh=mesh,
        in_specs=(
            P("blk", None, "tp"),
            P("blk", None, "tp"),
            P("blk", None, "tp"),
            P("blk", None, "tp"),
            P("tp", None),
            P("blk"),
            P("blk", None),
            P("blk"),
            P("blk"),
        ),
        out_specs=P("blk", None, "tp"),
        check_vma=False,
    )
```

```python
import functools

import jax
import jax.numpy as jnp
from jax import lax
from jax.experimental import pallas as pl
from jax.experimental.pallas import tpu as pltpu
from jax.sharding import PartitionSpec as P


TILE = 128
S_MAX = 2
GROUP = 64
SEG = 512
LOG2E = 1.4426950408889634
MASKED = -1e30
VMEM_LIMIT = 58 << 20


def group_softmax(n, qg, kx_ref, vx_ref, b, scale, hd):
    tops, outs = [], []
    for i in range(n):
        at = slice(i * SEG, (i + 1) * SEG)
        s = lax.dot_general(
            qg, kx_ref[b, at, :], (((1,), (1,)), ((), ())), preferred_element_type=jnp.float32
        )
        top = jnp.max(s, axis=1, keepdims=True)
        p = jnp.exp2((s - top) * scale).astype(jnp.bfloat16)
        tops.append(top)
        outs.append(jnp.dot(p, vx_ref[b, at, :], preferred_element_type=jnp.float32))
    if n == 1:
        acc = outs[0]
    else:
        top = functools.reduce(jnp.maximum, tops)
        acc = sum(o * jnp.exp2((t - top) * scale) for o, t in zip(outs, tops))
    return (acc[:, :hd] / acc[:, hd:]).astype(jnp.bfloat16)


def shard_order():
    me = lax.axis_index("tp")
    x, core = me // 2, me % 2
    return [2 * x + 1 - core, 2 * (1 - x) + 1 - core, 2 * (1 - x) + core, me]


def weight_copies(w_hbm, w_ref, sems):
    cols = w_ref.shape[2] // 2
    copies = []
    for s, shard in enumerate(shard_order()):
        src = w_hbm.at[:, pl.ds(pl.multiple_of(shard * cols, 128), cols)]
        into = w_ref.at[s // 2, :, pl.ds(s % 2 * cols, cols)]
        copies.append(pltpu.make_async_copy(src, into, sems.at[s]))
    return copies


def project(attn, residual, w_ref, w_copies, part_ref, mine_ref, outs, sems):
    count, cols = len(outs) // 3, mine_ref.shape[1]
    nodes = attn.shape[0] // count
    copies = [[] for _ in range(4)]
    for b in range(count):
        at = pl.ds(b * nodes, nodes)
        to = [outs[b].at[0], outs[b].at[1], outs[count + b]]
        for s in range(3):
            copies[s].append(pltpu.make_async_copy(part_ref.at[s, at], to[s], sems.at[b, s]))
        copies[3].append(pltpu.make_async_copy(mine_ref.at[at], outs[2 * count + b], sems.at[b, 3]))
    w_copies[0].wait()
    w_copies[1].wait()
    part = jnp.dot(attn, w_ref[0], preferred_element_type=jnp.float32)
    for s in range(2):
        part_ref[s] = part[:, s * cols : (s + 1) * cols].astype(jnp.bfloat16)
        for copy in copies[s]:
            copy.start()
    w_copies[2].wait()
    w_copies[3].wait()
    part = jnp.dot(attn, w_ref[1], preferred_element_type=jnp.float32)
    part_ref[2] = part[:, :cols].astype(jnp.bfloat16)
    mine_ref[...] = part[:, cols:] + residual().astype(jnp.float32)
    for copy in copies[2] + copies[3]:
        copy.start()
    return sum(copies, [])


def attend_kernel(
    ids, shipped, live_ref, q_hbm, k_hbm, v_hbm, hidden_hbm, tiles_hbm, w_hbm, *refs,
):
    made = len(ids) - shipped
    outs, refs = refs[: 3 * made + shipped], refs[3 * made + shipped :]
    (
        tiles_ref, hidden_ref, ship_ref, q_ref, w_ref, kx_ref, vx_ref, qx_ref, attn_ref, perm_ref,
        part_ref, mine_ref, segs_ref, sems, out_sems,
    ) = refs
    count, nodes, width = q_ref.shape
    places, hd = kx_ref.shape[1], kx_ref.shape[2] // 2
    heads = width // hd
    groups = nodes // GROUP
    rows = heads * GROUP
    scale = jnp.float32(hd**-0.5 * LOG2E)

    tiles_copy = pltpu.make_async_copy(tiles_hbm, tiles_ref, sems.at[3, 0])
    q_copies, k_copies, v_copies, hidden_copies = [], [], [], []
    for b, j in enumerate(ids):
        q_copies.append(pltpu.make_async_copy(q_hbm.at[j], q_ref.at[b], sems.at[0, b]))
        k_copies.append(
            pltpu.make_async_copy(k_hbm.at[j], kx_ref.at[b, :, pl.ds(0, hd)], sems.at[1, b])
        )
        v_copies.append(
            pltpu.make_async_copy(v_hbm.at[j], vx_ref.at[b, :, pl.ds(0, hd)], sems.at[2, b])
        )
        into = hidden_ref.at[pl.ds(b * nodes, nodes)]
        hidden_copies.append(pltpu.make_async_copy(hidden_hbm.at[j], into, sems.at[6, b]))
    w_copies = weight_copies(w_hbm, w_ref, sems.at[4])
    tiles_copy.start()
    for b in range(count):
        q_copies[b].start()
    for b in range(count):
        k_copies[b].start()
        v_copies[b].start()

    tile_of = lax.broadcasted_iota(jnp.int32, (places, hd), 0) // TILE
    lane_of = lax.broadcasted_iota(jnp.int32, (places, hd), 1)
    marks = jnp.where(tile_of == lane_of, 1.0, 0.0).astype(jnp.bfloat16)
    for b in range(count):
        kx_ref[b, :, hd:] = marks
        vx_ref[b, :, hd:] = jnp.ones((places, hd), jnp.bfloat16)
    attn_ref[...] = jnp.zeros_like(attn_ref)

    sub = lax.broadcasted_iota(jnp.int32, (nodes, nodes), 0)
    lane = lax.broadcasted_iota(jnp.int32, (nodes, nodes), 1)
    sub_f, lane_f = sub.astype(jnp.float32), lane.astype(jnp.float32)
    tiles_copy.wait()
    for b, j in enumerate(ids):
        live = live_ref[j]
        tiles_row = jnp.broadcast_to(tiles_ref[j : j + 1, :], (nodes, nodes))
        reach_row = jnp.where(lane < live, tiles_row, 0)
        key_row = (reach_row * nodes + (nodes - 1 - lane)).astype(jnp.float32)
        key_col = key_row.T
        rank_row = jnp.sum(jnp.where(key_col > key_row, 1.0, 0.0), axis=0, keepdims=True)
        rank_col = jnp.sum(jnp.where(key_row > key_col, 1.0, 0.0), axis=1, keepdims=True)
        alive = (rank_col == lane_f) & (sub < live)
        perm_ref[b] = jnp.where(alive, 1.0, 0.0).astype(jnp.bfloat16)
        to_sorted = rank_row == sub_f
        reach = jnp.sum(
            jnp.where(to_sorted, reach_row.astype(jnp.float32), 0.0), axis=1, keepdims=True
        )
        for g in range(groups):
            longest = jnp.max(reach[g * GROUP : (g + 1) * GROUP]).astype(jnp.int32)
            segs_ref[b * groups + g] = (longest * TILE + SEG - 1) // SEG
        hidden_from = (lane_f >= jnp.maximum(reach, 1.0)) & (lane < places // TILE)
        bias = jnp.where(hidden_from, MASKED, 0.0)[:, :hd].astype(jnp.bfloat16)
        q_copies[b].wait()
        q_sorted = jnp.dot(
            jnp.where(to_sorted, 1.0, 0.0).astype(jnp.bfloat16), q_ref[b],
            preferred_element_type=jnp.float32,
        ).astype(jnp.bfloat16)
        for g in range(groups):
            for h in range(heads):
                start = (b * groups + g) * rows + h * GROUP
                at = slice(start, start + GROUP)
                qx_ref[at, :hd] = q_sorted[g * GROUP : (g + 1) * GROUP, h * hd : (h + 1) * hd]
                qx_ref[at, hd:] = bias[g * GROUP : (g + 1) * GROUP]

    def alive_residual(b):
        row = lax.broadcasted_iota(jnp.int32, (nodes, hidden_ref.shape[1]), 0)
        residual = hidden_ref[b * nodes : (b + 1) * nodes, :]
        return jnp.where(row < live_ref[ids[b]], residual, jnp.zeros((), residual.dtype))

    ship_copies = []
    for b, j in enumerate(ids):
        k_copies[b].wait()
        v_copies[b].wait()
        if b == 0:
            for copy in hidden_copies + w_copies:
                copy.start()

        @pl.loop(0, (live_ref[j] + GROUP - 1) // GROUP)
        def _(g):
            at = pl.ds(pl.multiple_of((b * groups + g) * rows, GROUP), rows)
            out_at = pl.ds(pl.multiple_of(b * nodes + g * GROUP, GROUP), GROUP)
            segs = segs_ref[b * groups + g]

            def attend(n):
                mixed = group_softmax(n, qx_ref[at, :], kx_ref, vx_ref, b, scale, hd)
                for h in range(heads):
                    attn_ref[out_at, h * hd : (h + 1) * hd] = mixed[h * GROUP : (h + 1) * GROUP]

            def pick(low, high):
                if low == high:
                    attend(low)
                else:
                    half = (low + high) // 2
                    pl.when(segs <= half)(functools.partial(pick, low, half))
                    pl.when(segs > half)(functools.partial(pick, half + 1, high))

            pick(1, places // SEG)

        at = slice(b * nodes, (b + 1) * nodes)
        in_place = jnp.dot(
            perm_ref[b], attn_ref[at, :], preferred_element_type=jnp.float32
        ).astype(jnp.bfloat16)
        if b < shipped:
            ship_ref[0] = in_place
            hidden_copies[b].wait()
            ship_ref[1] = alive_residual(b)
            ship_copies.append(pltpu.make_async_copy(ship_ref, outs[3 * made], sems.at[3, 1]))
            ship_copies[0].start()
        else:
            attn_ref[at, :] = in_place

    def residual():
        for copy in hidden_copies[shipped:]:
            copy.wait()
        return jnp.concatenate([alive_residual(b) for b in range(shipped, count)], axis=0)

    out_copies = project(
        attn_ref[shipped * nodes :, :], residual, w_ref, w_copies, part_ref, mine_ref,
        outs[: 3 * made], out_sems,
    )
    for copy in ship_copies + out_copies:
        copy.wait()


def project_kernel(
    moved_hbm, w_hbm, send_hbm, keep_hbm, mine_hbm, moved_ref, w_ref, part_ref, mine_ref, sems,
    out_sems,
):
    moved_copy = pltpu.make_async_copy(moved_hbm, moved_ref, sems.at[2, 0])
    moved_copy.start()
    w_copies = weight_copies(w_hbm, w_ref, sems.at[0])
    for copy in w_copies:
        copy.start()
    moved_copy.wait()
    out_copies = project(
        moved_ref[0], lambda: moved_ref[1], w_ref, w_copies, part_ref, mine_ref,
        (send_hbm, keep_hbm, mine_hbm), out_sems,
    )
    for copy in out_copies:
        copy.wait()


def partial_shapes(count, rows, cols):
    return (
        [pltpu.VMEM((2, rows, cols), jnp.bfloat16)] * count
        + [pltpu.VMEM((rows, cols), jnp.bfloat16)] * count
        + [pltpu.VMEM((rows, cols), jnp.float32)] * count
    )


def attend_blocks(ids, shipped, q, k, v, hidden, tiles, live, w):
    _, nodes, width = q.shape
    places, hd = k.shape[1], k.shape[2]
    heads = width // hd
    cols = hidden.shape[2]
    count = len(ids)
    made = (count - shipped) * nodes
    bf16 = jnp.bfloat16
    outs = partial_shapes(count - shipped, nodes, cols)
    outs += [jax.ShapeDtypeStruct((2, nodes, cols), bf16)] * shipped
    anywhere = pl.BlockSpec(memory_space=pl.ANY)
    grid_spec = pltpu.PrefetchScalarGridSpec(
        num_scalar_prefetch=1,
        grid=(1,),
        in_specs=[anywhere] * 6,
        out_specs=[anywhere] * len(outs),
        scratch_shapes=[
            pltpu.VMEM(tiles.shape, jnp.int32),
            pltpu.VMEM((count * nodes, cols), bf16),
            pltpu.VMEM((2, nodes, cols), bf16),
            pltpu.VMEM((count, nodes, width), bf16),
            pltpu.VMEM((2, width, 2 * cols), bf16),
            pltpu.VMEM((count, places, 2 * hd), bf16),
            pltpu.VMEM((count, places, 2 * hd), bf16),
            pltpu.VMEM((count * heads * nodes, 2 * hd), bf16),
            pltpu.VMEM((count * nodes, width), bf16),
            pltpu.VMEM((count, nodes, nodes), bf16),
            pltpu.VMEM((3, made, cols), bf16),
            pltpu.VMEM((made, cols), jnp.float32),
            pltpu.SMEM((count * (nodes // GROUP),), jnp.int32),
            pltpu.SemaphoreType.DMA((7, max(4, count))),
            pltpu.SemaphoreType.DMA((count - shipped, 4)),
        ],
    )
    return pl.pallas_call(
        functools.partial(attend_kernel, ids, shipped),
        grid_spec=grid_spec,
        out_shape=outs,
        compiler_params=pltpu.CompilerParams(vmem_limit_bytes=VMEM_LIMIT),
        cost_estimate=pl.CostEstimate(
            flops=4 * count * nodes * width * places + 2 * made * width * w.shape[1],
            bytes_accessed=w.size * 2 + count * 4 * places * hd,
            transcendentals=count * nodes * heads * places,
        ),
    )(live, q, k, v, hidden, tiles, w)


def project_block(moved, w):
    _, nodes, cols = moved.shape
    width = w.shape[0]
    outs = partial_shapes(1, nodes, cols)
    anywhere = pl.BlockSpec(memory_space=pl.ANY)
    return pl.pallas_call(
        project_kernel,
        in_specs=[anywhere] * 2,
        out_specs=[anywhere] * len(outs),
        scratch_shapes=[
            pltpu.VMEM(moved.shape, jnp.bfloat16),
            pltpu.VMEM((2, width, 2 * cols), jnp.bfloat16),
            pltpu.VMEM((3, nodes, cols), jnp.bfloat16),
            pltpu.VMEM((nodes, cols), jnp.float32),
            pltpu.SemaphoreType.DMA((3, 4)),
            pltpu.SemaphoreType.DMA((1, 4)),
        ],
        out_shape=outs,
        compiler_params=pltpu.CompilerParams(vmem_limit_bytes=VMEM_LIMIT),
        cost_estimate=pl.CostEstimate(
            flops=2 * nodes * width * w.shape[1], bytes_accessed=w.size * 2, transcendentals=0
        ),
    )(moved, w)


def on_device(
    kv_keys, kv_values, queries, hidden, out_weight, block_live, node_tiles, left_count, right_count
):
    blocks, nodes, _ = queries.shape
    tp = lax.axis_size("tp")
    ring = lax.axis_size("blk")
    to_mate = [(i, i ^ 1) for i in range(tp)]
    to_across = [(i, i ^ 2) for i in range(tp)]
    to_next = [(i, (i + 1) % ring) for i in range(ring)]
    to_prev = [(i, (i - 1) % ring) for i in range(ring)]
    bf16, wide = jnp.bfloat16, jnp.float32

    left, right = left_count[0], right_count[0]
    zero = jnp.zeros((), jnp.bfloat16)

    def attend(ids, shipped):
        return attend_blocks(
            ids, shipped, queries, kv_keys, kv_values, hidden, node_tiles, block_live,
            out_weight,
        )

    def sum_start(send, keep):
        got = lax.ppermute(send, "tp", to_mate)
        across = (keep.astype(wide) + got[1].astype(wide)).astype(bf16)
        return got[0], lax.ppermute(across, "tp", to_across)

    def total(mine, mates, other):
        return mine + mates.astype(wide) + other.astype(wide)

    last = blocks - 1
    out = jnp.zeros((blocks + 2 * S_MAX, nodes, hidden.shape[2]), bf16)
    send0, send1, keep0, keep1, mine0, mine1, ship = attend((last, 0, 1), 1)
    moved = lax.ppermute(ship, "blk", to_next)
    mates0, other0 = sum_start(send0, keep0)
    mates1, other1 = sum_start(send1, keep1)
    send2, keep2, mine2 = attend((2,), 0)
    mates2, other2 = sum_start(send2, keep2)
    send3, keep3, mine3 = project_block(moved, out_weight)
    mates3, other3 = sum_start(send3, keep3)

    def masked(value, kept):
        return jnp.where(kept, value.astype(bf16), zero)

    from_next0 = lax.ppermute(total(mine0, mates0, other0).astype(bf16), "blk", to_prev)
    result = total(mine1, mates1, other1)
    own1 = masked(result, (left <= 1) & (1 < blocks - right))
    from_next1 = lax.ppermute(masked(result, 1 < left), "blk", to_prev)
    result = total(mine2, mates2, other2)
    own2 = masked(result, (left <= 2) & (2 < blocks - right))
    from_prev = lax.ppermute(masked(result, blocks - 2 <= right), "blk", to_next)
    out = out.at[S_MAX + 1].set(own1)
    out = out.at[S_MAX + 2].set(own2)
    out = out.at[S_MAX + blocks].set(from_next0)
    out = out.at[S_MAX + blocks + 1].set(from_next1)
    out = out.at[1].set(total(mine3, mates3, other3).astype(bf16))
    return out.at[0].set(from_prev)


def solution(mesh):
    return jax.shard_map(
        on_device,
        mesh=mesh,
        in_specs=(
            P("blk", None, "tp"),
            P("blk", None, "tp"),
            P("blk", None, "tp"),
            P("blk", None, "tp"),
            P("tp", None),
            P("blk"),
            P("blk", None),
            P("blk"),
            P("blk"),
        ),
        out_specs=P("blk", None, "tp"),
        check_vma=False,
    )
```

```python
import functools

import jax
import jax.numpy as jnp
from jax import lax
from jax.experimental import pallas as pl
from jax.experimental.pallas import tpu as pltpu
from jax.sharding import PartitionSpec as P


TILE = 128
S_MAX = 2
GROUP = 64
SEG = 512
LOG2E = 1.4426950408889634
MASKED = -1e30
VMEM_LIMIT = 44 << 20


def group_softmax(n, qg, kx_ref, vx_ref, b, scale, hd):
    tops, outs = [], []
    for i in range(n):
        at = slice(i * SEG, (i + 1) * SEG)
        s = lax.dot_general(
            qg, kx_ref[b, at, :], (((1,), (1,)), ((), ())), preferred_element_type=jnp.float32
        )
        top = jnp.max(s, axis=1, keepdims=True)
        p = jnp.exp2((s - top) * scale).astype(jnp.bfloat16)
        tops.append(top)
        outs.append(jnp.dot(p, vx_ref[b, at, :], preferred_element_type=jnp.float32))
    if n == 1:
        acc = outs[0]
    else:
        top = functools.reduce(jnp.maximum, tops)
        acc = sum(o * jnp.exp2((t - top) * scale) for o, t in zip(outs, tops))
    return (acc[:, :hd] / acc[:, hd:]).astype(jnp.bfloat16)


def shard_order():
    me = lax.axis_index("tp")
    x, core = me // 2, me % 2
    return [2 * x + 1 - core, 2 * (1 - x) + 1 - core, 2 * (1 - x) + core, me]


def weight_copies(w_hbm, w_ref, sems):
    cols = w_ref.shape[2] // 2
    copies = []
    for s, shard in enumerate(shard_order()):
        src = w_hbm.at[:, pl.ds(pl.multiple_of(shard * cols, 128), cols)]
        into = w_ref.at[s // 2, :, pl.ds(s % 2 * cols, cols)]
        copies.append(pltpu.make_async_copy(src, into, sems.at[s]))
    return copies


def project(attn, residual, w_ref, w_copies, outs):
    count = len(outs) // 3
    nodes, cols = outs[-1].shape
    for copy in w_copies[:2]:
        copy.wait()
    part = jnp.dot(attn, w_ref[0], preferred_element_type=jnp.float32)
    for b in range(count):
        at = slice(b * nodes, (b + 1) * nodes)
        for s in range(2):
            outs[b][s] = part[at, s * cols : (s + 1) * cols].astype(jnp.bfloat16)
    for copy in w_copies[2:]:
        copy.wait()
    part = jnp.dot(attn, w_ref[1], preferred_element_type=jnp.float32)
    rest = residual().astype(jnp.float32)
    for b in range(count):
        at = slice(b * nodes, (b + 1) * nodes)
        outs[count + b][...] = part[at, :cols].astype(jnp.bfloat16)
        outs[2 * count + b][...] = part[at, cols:] + rest[at]


def attend_kernel(
    ids, shipped, live_ref, q_hbm, k_hbm, v_hbm, hidden_hbm, tiles_hbm, w_hbm, *refs,
):
    made = len(ids) - shipped
    extra = 2 if shipped else 0
    outs, refs = refs[: 3 * made + extra], refs[3 * made + extra :]
    (
        tiles_ref, hidden_ref, q_ref, kx_ref, vx_ref, qx_ref, attn_ref, perm_ref,
        segs_ref, sems,
    ) = refs
    count, nodes, width = q_ref.shape
    places, hd = kx_ref.shape[1], kx_ref.shape[2] // 2
    heads = width // hd
    groups = nodes // GROUP
    rows = heads * GROUP
    scale = jnp.float32(hd**-0.5 * LOG2E)

    tiles_copy = pltpu.make_async_copy(tiles_hbm, tiles_ref, sems.at[3, 0])
    q_copies, k_copies, v_copies, hidden_copies = [], [], [], []
    for b, j in enumerate(ids):
        q_copies.append(pltpu.make_async_copy(q_hbm.at[j], q_ref.at[b], sems.at[0, b]))
        k_copies.append(
            pltpu.make_async_copy(k_hbm.at[j], kx_ref.at[b, :, pl.ds(0, hd)], sems.at[1, b])
        )
        v_copies.append(
            pltpu.make_async_copy(v_hbm.at[j], vx_ref.at[b, :, pl.ds(0, hd)], sems.at[2, b])
        )
        into = hidden_ref.at[pl.ds(b * nodes, nodes)]
        hidden_copies.append(pltpu.make_async_copy(hidden_hbm.at[j], into, sems.at[6, b]))
    w_ref = outs[3 * made + 1] if shipped else w_hbm
    w_copies = weight_copies(w_hbm, w_ref, sems.at[4]) if shipped else []
    tiles_copy.start()
    for b in range(count):
        q_copies[b].start()
    for b in range(count):
        k_copies[b].start()
        v_copies[b].start()

    tile_of = lax.broadcasted_iota(jnp.int32, (places, hd), 0) // TILE
    lane_of = lax.broadcasted_iota(jnp.int32, (places, hd), 1)
    marks = jnp.where(tile_of == lane_of, 1.0, 0.0).astype(jnp.bfloat16)
    for b in range(count):
        kx_ref[b, :, hd:] = marks
        vx_ref[b, :, hd:] = jnp.ones((places, hd), jnp.bfloat16)
    attn_ref[...] = jnp.zeros_like(attn_ref)

    sub = lax.broadcasted_iota(jnp.int32, (nodes, nodes), 0)
    lane = lax.broadcasted_iota(jnp.int32, (nodes, nodes), 1)
    sub_f, lane_f = sub.astype(jnp.float32), lane.astype(jnp.float32)
    tiles_copy.wait()
    for b, j in enumerate(ids):
        live = live_ref[j]
        tiles_row = jnp.broadcast_to(tiles_ref[j : j + 1, :], (nodes, nodes))
        reach_row = jnp.where(lane < live, tiles_row, 0)
        key_row = (reach_row * nodes + (nodes - 1 - lane)).astype(jnp.float32)
        key_col = key_row.T
        rank_row = jnp.sum(jnp.where(key_col > key_row, 1.0, 0.0), axis=0, keepdims=True)
        rank_col = jnp.sum(jnp.where(key_row > key_col, 1.0, 0.0), axis=1, keepdims=True)
        alive = (rank_col == lane_f) & (sub < live)
        perm_ref[b] = jnp.where(alive, 1.0, 0.0).astype(jnp.bfloat16)
        to_sorted = rank_row == sub_f
        reach = jnp.sum(
            jnp.where(to_sorted, reach_row.astype(jnp.float32), 0.0), axis=1, keepdims=True
        )
        for g in range(groups):
            longest = jnp.max(reach[g * GROUP : (g + 1) * GROUP]).astype(jnp.int32)
            segs_ref[b * groups + g] = (longest * TILE + SEG - 1) // SEG
        hidden_from = (lane_f >= jnp.maximum(reach, 1.0)) & (lane < places // TILE)
        bias = jnp.where(hidden_from, MASKED, 0.0)[:, :hd].astype(jnp.bfloat16)
        q_copies[b].wait()
        q_sorted = jnp.dot(
            jnp.where(to_sorted, 1.0, 0.0).astype(jnp.bfloat16), q_ref[b],
            preferred_element_type=jnp.float32,
        ).astype(jnp.bfloat16)
        for g in range(groups):
            for h in range(heads):
                start = (b * groups + g) * rows + h * GROUP
                at = slice(start, start + GROUP)
                qx_ref[at, :hd] = q_sorted[g * GROUP : (g + 1) * GROUP, h * hd : (h + 1) * hd]
                qx_ref[at, hd:] = bias[g * GROUP : (g + 1) * GROUP]

    def alive_residual(b):
        row = lax.broadcasted_iota(jnp.int32, (nodes, hidden_ref.shape[1]), 0)
        residual = hidden_ref[b * nodes : (b + 1) * nodes, :]
        return jnp.where(row < live_ref[ids[b]], residual, jnp.zeros((), residual.dtype))

    for b, j in enumerate(ids):
        k_copies[b].wait()
        v_copies[b].wait()
        if b == 0:
            for copy in hidden_copies + w_copies:
                copy.start()

        @pl.loop(0, (live_ref[j] + GROUP - 1) // GROUP)
        def _(g):
            at = pl.ds(pl.multiple_of((b * groups + g) * rows, GROUP), rows)
            out_at = pl.ds(pl.multiple_of(b * nodes + g * GROUP, GROUP), GROUP)
            segs = segs_ref[b * groups + g]

            def attend(n):
                mixed = group_softmax(n, qx_ref[at, :], kx_ref, vx_ref, b, scale, hd)
                for h in range(heads):
                    attn_ref[out_at, h * hd : (h + 1) * hd] = mixed[h * GROUP : (h + 1) * GROUP]

            def pick(low, high):
                if low == high:
                    attend(low)
                else:
                    half = (low + high) // 2
                    pl.when(segs <= half)(functools.partial(pick, low, half))
                    pl.when(segs > half)(functools.partial(pick, half + 1, high))

            pick(1, places // SEG)

        at = slice(b * nodes, (b + 1) * nodes)
        in_place = jnp.dot(
            perm_ref[b], attn_ref[at, :], preferred_element_type=jnp.float32
        ).astype(jnp.bfloat16)
        if b < shipped:
            outs[3 * made][0] = in_place
            hidden_copies[b].wait()
            outs[3 * made][1] = alive_residual(b)
        else:
            attn_ref[at, :] = in_place

    def residual():
        for copy in hidden_copies[shipped:]:
            copy.wait()
        return jnp.concatenate([alive_residual(b) for b in range(shipped, count)], axis=0)

    project(attn_ref[shipped * nodes :, :], residual, w_ref, w_copies, outs[: 3 * made])


def project_kernel(moved_ref, w_ref, *outs):
    project(moved_ref[0], lambda: moved_ref[1], w_ref, [], outs)


def partial_shapes(count, rows, cols):
    return (
        [pltpu.VMEM((2, rows, cols), jnp.bfloat16)] * count
        + [pltpu.VMEM((rows, cols), jnp.bfloat16)] * count
        + [pltpu.VMEM((rows, cols), jnp.float32)] * count
    )


def attend_blocks(ids, shipped, q, k, v, hidden, tiles, live, w):
    _, nodes, width = q.shape
    places, hd = k.shape[1], k.shape[2]
    heads = width // hd
    cols = hidden.shape[2]
    count = len(ids)
    made = (count - shipped) * nodes
    bf16 = jnp.bfloat16
    outs = partial_shapes(count - shipped, nodes, cols)
    in_vmem = pl.BlockSpec(memory_space=pltpu.VMEM)
    if shipped:
        outs += [pltpu.VMEM((2, nodes, cols), bf16), pltpu.VMEM((2, width, 2 * cols), bf16)]
    anywhere = pl.BlockSpec(memory_space=pl.ANY)
    grid_spec = pltpu.PrefetchScalarGridSpec(
        num_scalar_prefetch=1,
        grid=(),
        in_specs=[anywhere] * 5 + [anywhere if shipped else in_vmem],
        out_specs=[in_vmem] * len(outs),
        scratch_shapes=[
            pltpu.VMEM(tiles.shape, jnp.int32),
            pltpu.VMEM((count * nodes, cols), bf16),
            pltpu.VMEM((count, nodes, width), bf16),
            pltpu.VMEM((count, places, 2 * hd), bf16),
            pltpu.VMEM((count, places, 2 * hd), bf16),
            pltpu.VMEM((count * heads * nodes, 2 * hd), bf16),
            pltpu.VMEM((count * nodes, width), bf16),
            pltpu.VMEM((count, nodes, nodes), bf16),
            pltpu.SMEM((count * (nodes // GROUP),), jnp.int32),
            pltpu.SemaphoreType.DMA((7, max(4, count))),
        ],
    )
    return pl.pallas_call(
        functools.partial(attend_kernel, ids, shipped),
        grid_spec=grid_spec,
        out_shape=outs,
        compiler_params=pltpu.CompilerParams(vmem_limit_bytes=VMEM_LIMIT),
        cost_estimate=pl.CostEstimate(
            flops=4 * count * nodes * width * places + 8 * made * width * cols,
            bytes_accessed=w.size * 2 + count * 4 * places * hd,
            transcendentals=count * nodes * heads * places,
        ),
    )(live, q, k, v, hidden, tiles, w)


def project_block(moved, w):
    _, nodes, cols = moved.shape
    outs = partial_shapes(1, nodes, cols)
    in_vmem = pl.BlockSpec(memory_space=pltpu.VMEM)
    return pl.pallas_call(
        project_kernel,
        in_specs=[in_vmem] * 2,
        out_specs=[in_vmem] * len(outs),
        out_shape=outs,
        compiler_params=pltpu.CompilerParams(vmem_limit_bytes=VMEM_LIMIT),
        cost_estimate=pl.CostEstimate(
            flops=2 * nodes * w.size * 2, bytes_accessed=w.size * 2, transcendentals=0
        ),
    )(moved, w)


def on_device(
    kv_keys, kv_values, queries, hidden, out_weight, block_live, node_tiles, left_count, right_count
):
    blocks, nodes, _ = queries.shape
    tp = lax.axis_size("tp")
    ring = lax.axis_size("blk")
    to_mate = [(i, i ^ 1) for i in range(tp)]
    to_across = [(i, i ^ 2) for i in range(tp)]
    to_next = [(i, (i + 1) % ring) for i in range(ring)]
    to_prev = [(i, (i - 1) % ring) for i in range(ring)]
    bf16, wide = jnp.bfloat16, jnp.float32

    left, right = left_count[0], right_count[0]
    zero = jnp.zeros((), jnp.bfloat16)

    in_hbm = [kv_keys, kv_values, queries, hidden, out_weight, node_tiles]
    kv_keys, kv_values, queries, hidden, out_weight, node_tiles = [
        pltpu.with_memory_space_constraint(a, pltpu.HBM) for a in in_hbm
    ]

    def attend(ids, shipped, weight):
        return attend_blocks(
            ids, shipped, queries, kv_keys, kv_values, hidden, node_tiles, block_live,
            weight,
        )

    def sum_start(send, keep):
        got = lax.ppermute(send, "tp", to_mate)
        across = (keep.astype(wide) + got[1].astype(wide)).astype(bf16)
        return got[0], lax.ppermute(across, "tp", to_across)

    def total(mine, mates, other):
        return mine + mates.astype(wide) + other.astype(wide)

    last = blocks - 1
    out = jnp.zeros((blocks + 2 * S_MAX, nodes, hidden.shape[2]), bf16)
    send0, send1, keep0, keep1, mine0, mine1, ship, weight = attend((last, 0, 1), 1, out_weight)
    moved = lax.ppermute(ship, "blk", to_next)
    mates0, other0 = sum_start(send0, keep0)
    mates1, other1 = sum_start(send1, keep1)
    send2, keep2, mine2 = attend((2,), 0, weight)
    mates2, other2 = sum_start(send2, keep2)
    send3, keep3, mine3 = project_block(moved, weight)
    mates3, other3 = sum_start(send3, keep3)

    def masked(value, kept):
        return jnp.where(kept, value.astype(bf16), zero)

    from_next0 = lax.ppermute(total(mine0, mates0, other0).astype(bf16), "blk", to_prev)
    result = total(mine1, mates1, other1)
    own1 = masked(result, (left <= 1) & (1 < blocks - right))
    from_next1 = lax.ppermute(masked(result, 1 < left), "blk", to_prev)
    result = total(mine2, mates2, other2)
    own2 = masked(result, (left <= 2) & (2 < blocks - right))
    from_prev = lax.ppermute(masked(result, blocks - 2 <= right), "blk", to_next)
    out = out.at[S_MAX + 1].set(own1)
    out = out.at[S_MAX + 2].set(own2)
    out = out.at[S_MAX + blocks].set(from_next0)
    out = out.at[S_MAX + blocks + 1].set(from_next1)
    out = out.at[1].set(total(mine3, mates3, other3).astype(bf16))
    return out.at[0].set(from_prev)


def solution(mesh):
    return jax.shard_map(
        on_device,
        mesh=mesh,
        in_specs=(
            P("blk", None, "tp"),
            P("blk", None, "tp"),
            P("blk", None, "tp"),
            P("blk", None, "tp"),
            P("tp", None),
            P("blk"),
            P("blk", None),
            P("blk"),
            P("blk"),
        ),
        out_specs=P("blk", None, "tp"),
        check_vma=False,
    )
```

```python
import functools

import jax
import jax.numpy as jnp
from jax import lax
from jax.experimental import pallas as pl
from jax.experimental.pallas import tpu as pltpu
from jax.sharding import PartitionSpec as P


TILE = 128
S_MAX = 2
GROUP = 64
SEG = 512
LOG2E = 1.4426950408889634
MASKED = -1e30
VMEM_LIMIT = 44 << 20


def group_softmax(n, qg, kx_ref, vx_ref, b, scale, hd):
    tops, outs = [], []
    for i in range(n):
        at = slice(i * SEG, (i + 1) * SEG)
        s = lax.dot_general(
            qg, kx_ref[b, at, :], (((1,), (1,)), ((), ())), preferred_element_type=jnp.float32
        )
        top = jnp.max(s, axis=1, keepdims=True)
        p = jnp.exp2((s - top) * scale).astype(jnp.bfloat16)
        tops.append(top)
        outs.append(jnp.dot(p, vx_ref[b, at, :], preferred_element_type=jnp.float32))
    if n == 1:
        acc = outs[0]
    else:
        top = functools.reduce(jnp.maximum, tops)
        acc = sum(o * jnp.exp2((t - top) * scale) for o, t in zip(outs, tops))
    return (acc[:, :hd] / acc[:, hd:]).astype(jnp.bfloat16)


def shard_order():
    me = lax.axis_index("tp")
    x, core = me // 2, me % 2
    return [2 * x + 1 - core, 2 * (1 - x) + 1 - core, 2 * (1 - x) + core, me]


def weight_copies(w_hbm, w_ref, sems):
    cols = w_ref.shape[2] // 2
    copies = []
    for s, shard in enumerate(shard_order()):
        src = w_hbm.at[:, pl.ds(pl.multiple_of(shard * cols, 128), cols)]
        into = w_ref.at[s // 2, :, pl.ds(s % 2 * cols, cols)]
        copies.append(pltpu.make_async_copy(src, into, sems.at[s]))
    return copies


def project(attn, residual, w_ref, w_copies, outs):
    count = len(outs) // 3
    nodes, cols = outs[-1].shape
    for copy in w_copies[:2]:
        copy.wait()
    part = jnp.dot(attn, w_ref[0], preferred_element_type=jnp.float32)
    for b in range(count):
        at = slice(b * nodes, (b + 1) * nodes)
        for s in range(2):
            outs[b][s] = part[at, s * cols : (s + 1) * cols].astype(jnp.bfloat16)
    for copy in w_copies[2:]:
        copy.wait()
    part = jnp.dot(attn, w_ref[1], preferred_element_type=jnp.float32)
    rest = residual().astype(jnp.float32)
    for b in range(count):
        at = slice(b * nodes, (b + 1) * nodes)
        outs[count + b][...] = part[at, :cols].astype(jnp.bfloat16)
        outs[2 * count + b][...] = part[at, cols:] + rest[at]


def attend_kernel(
    ids, shipped, live_ref, q_hbm, k_hbm, v_hbm, hidden_hbm, tiles_hbm, w_hbm, *refs,
):
    made = len(ids) - shipped
    extra = 2 if shipped else 0
    outs, refs = refs[: 3 * made + extra], refs[3 * made + extra :]
    (
        tiles_ref, hidden_ref, q_ref, kx_ref, vx_ref, qx_ref, attn_ref, perm_ref,
        segs_ref, sems,
    ) = refs
    count, nodes, width = q_ref.shape
    places, hd = kx_ref.shape[1], kx_ref.shape[2] // 2
    heads = width // hd
    groups = nodes // GROUP
    rows = heads * GROUP
    scale = jnp.float32(hd**-0.5 * LOG2E)

    tiles_copy = pltpu.make_async_copy(tiles_hbm, tiles_ref, sems.at[3, 0])
    q_copies, k_copies, v_copies, hidden_copies = [], [], [], []
    for b, j in enumerate(ids):
        q_copies.append(pltpu.make_async_copy(q_hbm.at[j], q_ref.at[b], sems.at[0, b]))
        k_copies.append(
            pltpu.make_async_copy(k_hbm.at[j], kx_ref.at[b, :, pl.ds(0, hd)], sems.at[1, b])
        )
        v_copies.append(
            pltpu.make_async_copy(v_hbm.at[j], vx_ref.at[b, :, pl.ds(0, hd)], sems.at[2, b])
        )
        into = hidden_ref.at[pl.ds(b * nodes, nodes)]
        hidden_copies.append(pltpu.make_async_copy(hidden_hbm.at[j], into, sems.at[6, b]))
    w_ref = outs[3 * made + 1] if shipped else w_hbm
    w_copies = weight_copies(w_hbm, w_ref, sems.at[4]) if shipped else []
    tiles_copy.start()
    for b in range(count):
        q_copies[b].start()
    for b in range(count):
        k_copies[b].start()
        v_copies[b].start()

    tile_of = lax.broadcasted_iota(jnp.int32, (places, hd), 0) // TILE
    lane_of = lax.broadcasted_iota(jnp.int32, (places, hd), 1)
    marks = jnp.where(tile_of == lane_of, 1.0, 0.0).astype(jnp.bfloat16)
    for b in range(count):
        kx_ref[b, :, hd:] = marks
        vx_ref[b, :, hd:] = jnp.ones((places, hd), jnp.bfloat16)
    attn_ref[...] = jnp.zeros_like(attn_ref)

    sub = lax.broadcasted_iota(jnp.int32, (nodes, nodes), 0)
    lane = lax.broadcasted_iota(jnp.int32, (nodes, nodes), 1)
    sub_f, lane_f = sub.astype(jnp.float32), lane.astype(jnp.float32)
    tiles_copy.wait()
    for b, j in enumerate(ids):
        live = live_ref[j]
        tiles_row = jnp.broadcast_to(tiles_ref[j : j + 1, :], (nodes, nodes))
        reach_row = jnp.where(lane < live, tiles_row, 0)
        key_row = (reach_row * nodes + (nodes - 1 - lane)).astype(jnp.float32)
        key_col = key_row.T
        rank_row = jnp.sum(jnp.where(key_col > key_row, 1.0, 0.0), axis=0, keepdims=True)
        rank_col = jnp.sum(jnp.where(key_row > key_col, 1.0, 0.0), axis=1, keepdims=True)
        alive = (rank_col == lane_f) & (sub < live)
        perm_ref[b] = jnp.where(alive, 1.0, 0.0).astype(jnp.bfloat16)
        to_sorted = rank_row == sub_f
        reach = jnp.sum(
            jnp.where(to_sorted, reach_row.astype(jnp.float32), 0.0), axis=1, keepdims=True
        )
        for g in range(groups):
            longest = jnp.max(reach[g * GROUP : (g + 1) * GROUP]).astype(jnp.int32)
            segs_ref[b * groups + g] = (longest * TILE + SEG - 1) // SEG
        hidden_from = (lane_f >= jnp.maximum(reach, 1.0)) & (lane < places // TILE)
        bias = jnp.where(hidden_from, MASKED, 0.0)[:, :hd].astype(jnp.bfloat16)
        q_copies[b].wait()
        q_sorted = jnp.dot(
            jnp.where(to_sorted, 1.0, 0.0).astype(jnp.bfloat16), q_ref[b],
            preferred_element_type=jnp.float32,
        ).astype(jnp.bfloat16)
        for g in range(groups):
            for h in range(heads):
                start = (b * groups + g) * rows + h * GROUP
                at = slice(start, start + GROUP)
                qx_ref[at, :hd] = q_sorted[g * GROUP : (g + 1) * GROUP, h * hd : (h + 1) * hd]
                qx_ref[at, hd:] = bias[g * GROUP : (g + 1) * GROUP]

    def alive_residual(b):
        row = lax.broadcasted_iota(jnp.int32, (nodes, hidden_ref.shape[1]), 0)
        residual = hidden_ref[b * nodes : (b + 1) * nodes, :]
        return jnp.where(row < live_ref[ids[b]], residual, jnp.zeros((), residual.dtype))

    for b, j in enumerate(ids):
        k_copies[b].wait()
        v_copies[b].wait()
        if b == 0:
            for copy in hidden_copies + w_copies:
                copy.start()

        @pl.loop(0, (live_ref[j] + GROUP - 1) // GROUP)
        def _(g):
            at = pl.ds(pl.multiple_of((b * groups + g) * rows, GROUP), rows)
            out_at = pl.ds(pl.multiple_of(b * nodes + g * GROUP, GROUP), GROUP)
            segs = segs_ref[b * groups + g]

            def attend(n):
                mixed = group_softmax(n, qx_ref[at, :], kx_ref, vx_ref, b, scale, hd)
                for h in range(heads):
                    attn_ref[out_at, h * hd : (h + 1) * hd] = mixed[h * GROUP : (h + 1) * GROUP]

            def pick(low, high):
                if low == high:
                    attend(low)
                else:
                    half = (low + high) // 2
                    pl.when(segs <= half)(functools.partial(pick, low, half))
                    pl.when(segs > half)(functools.partial(pick, half + 1, high))

            pick(1, places // SEG)

        at = slice(b * nodes, (b + 1) * nodes)
        in_place = jnp.dot(
            perm_ref[b], attn_ref[at, :], preferred_element_type=jnp.float32
        ).astype(jnp.bfloat16)
        if b < shipped:
            outs[3 * made][0] = in_place
            hidden_copies[b].wait()
            outs[3 * made][1] = alive_residual(b)
        else:
            attn_ref[at, :] = in_place

    def residual():
        for copy in hidden_copies[shipped:]:
            copy.wait()
        return jnp.concatenate([alive_residual(b) for b in range(shipped, count)], axis=0)

    project(attn_ref[shipped * nodes :, :], residual, w_ref, w_copies, outs[: 3 * made])


def project_kernel(moved_ref, w_ref, *outs):
    project(moved_ref[0], lambda: moved_ref[1], w_ref, [], outs)


def partial_shapes(count, rows, cols):
    return (
        [pltpu.VMEM((2, rows, cols), jnp.bfloat16)] * count
        + [pltpu.VMEM((rows, cols), jnp.bfloat16)] * count
        + [pltpu.VMEM((rows, cols), jnp.float32)] * count
    )


def attend_blocks(ids, shipped, q, k, v, hidden, tiles, live, w):
    _, nodes, width = q.shape
    places, hd = k.shape[1], k.shape[2]
    heads = width // hd
    cols = hidden.shape[2]
    count = len(ids)
    made = (count - shipped) * nodes
    bf16 = jnp.bfloat16
    outs = partial_shapes(count - shipped, nodes, cols)
    in_vmem = pl.BlockSpec(memory_space=pltpu.VMEM)
    if shipped:
        outs += [pltpu.VMEM((2, nodes, cols), bf16), pltpu.VMEM((2, width, 2 * cols), bf16)]
    anywhere = pl.BlockSpec(memory_space=pl.ANY)
    grid_spec = pltpu.PrefetchScalarGridSpec(
        num_scalar_prefetch=1,
        grid=(),
        in_specs=[anywhere] * 5 + [anywhere if shipped else in_vmem],
        out_specs=[in_vmem] * len(outs),
        scratch_shapes=[
            pltpu.VMEM(tiles.shape, jnp.int32),
            pltpu.VMEM((count * nodes, cols), bf16),
            pltpu.VMEM((count, nodes, width), bf16),
            pltpu.VMEM((count, places, 2 * hd), bf16),
            pltpu.VMEM((count, places, 2 * hd), bf16),
            pltpu.VMEM((count * heads * nodes, 2 * hd), bf16),
            pltpu.VMEM((count * nodes, width), bf16),
            pltpu.VMEM((count, nodes, nodes), bf16),
            pltpu.SMEM((count * (nodes // GROUP),), jnp.int32),
            pltpu.SemaphoreType.DMA((7, max(4, count))),
        ],
    )
    return pl.pallas_call(
        functools.partial(attend_kernel, ids, shipped),
        grid_spec=grid_spec,
        out_shape=outs,
        compiler_params=pltpu.CompilerParams(vmem_limit_bytes=VMEM_LIMIT),
        cost_estimate=pl.CostEstimate(
            flops=4 * count * nodes * width * places + 8 * made * width * cols,
            bytes_accessed=w.size * 2 + count * 4 * places * hd,
            transcendentals=count * nodes * heads * places,
        ),
    )(live, q, k, v, hidden, tiles, w)


def project_block(moved, w):
    _, nodes, cols = moved.shape
    outs = partial_shapes(1, nodes, cols)
    in_vmem = pl.BlockSpec(memory_space=pltpu.VMEM)
    return pl.pallas_call(
        project_kernel,
        in_specs=[in_vmem] * 2,
        out_specs=[in_vmem] * len(outs),
        out_shape=outs,
        compiler_params=pltpu.CompilerParams(vmem_limit_bytes=VMEM_LIMIT),
        cost_estimate=pl.CostEstimate(
            flops=2 * nodes * w.size * 2, bytes_accessed=w.size * 2, transcendentals=0
        ),
    )(moved, w)


def on_device(
    kv_keys, kv_values, queries, hidden, out_weight, block_live, node_tiles, left_count, right_count
):
    blocks, nodes, _ = queries.shape
    tp = lax.axis_size("tp")
    ring = lax.axis_size("blk")
    to_mate = [(i, i ^ 1) for i in range(tp)]
    to_across = [(i, i ^ 2) for i in range(tp)]
    to_next = [(i, (i + 1) % ring) for i in range(ring)]
    to_prev = [(i, (i - 1) % ring) for i in range(ring)]
    bf16, wide = jnp.bfloat16, jnp.float32

    left, right = left_count[0], right_count[0]
    zero = jnp.zeros((), jnp.bfloat16)

    in_hbm = [kv_keys, kv_values, queries, hidden, out_weight, node_tiles, block_live]
    (
        kv_keys, kv_values, queries, hidden, out_weight, node_tiles, block_live
    ) = [
        pltpu.with_memory_space_constraint(a, pltpu.HBM) for a in in_hbm
    ]

    def attend(ids, shipped, weight):
        return attend_blocks(
            ids, shipped, queries, kv_keys, kv_values, hidden, node_tiles, block_live,
            weight,
        )

    def sum_start(send, keep):
        got = lax.ppermute(send, "tp", to_mate)
        across = (keep.astype(wide) + got[1].astype(wide)).astype(bf16)
        return got[0], lax.ppermute(across, "tp", to_across)

    def total(mine, mates, other):
        return mine + mates.astype(wide) + other.astype(wide)

    last = blocks - 1
    out = jnp.zeros((blocks + 2 * S_MAX, nodes, hidden.shape[2]), bf16)
    send0, send1, keep0, keep1, mine0, mine1, ship, weight = attend((last, 0, 1), 1, out_weight)
    moved = lax.ppermute(ship, "blk", to_next)
    mates0, other0 = sum_start(send0, keep0)
    mates1, other1 = sum_start(send1, keep1)
    send2, keep2, mine2 = attend((2,), 0, weight)
    mates2, other2 = sum_start(send2, keep2)
    send3, keep3, mine3 = project_block(moved, weight)
    mates3, other3 = sum_start(send3, keep3)

    def masked(value, kept):
        return jnp.where(kept, value.astype(bf16), zero)

    from_next0 = lax.ppermute(total(mine0, mates0, other0).astype(bf16), "blk", to_prev)
    result = total(mine1, mates1, other1)
    own1 = masked(result, (left <= 1) & (1 < blocks - right))
    from_next1 = lax.ppermute(masked(result, 1 < left), "blk", to_prev)
    result = total(mine2, mates2, other2)
    own2 = masked(result, (left <= 2) & (2 < blocks - right))
    from_prev = lax.ppermute(masked(result, blocks - 2 <= right), "blk", to_next)
    out = out.at[S_MAX + 1].set(own1)
    out = out.at[S_MAX + 2].set(own2)
    out = out.at[S_MAX + blocks].set(from_next0)
    out = out.at[S_MAX + blocks + 1].set(from_next1)
    out = out.at[1].set(total(mine3, mates3, other3).astype(bf16))
    return out.at[0].set(from_prev)


def solution(mesh):
    return jax.shard_map(
        on_device,
        mesh=mesh,
        in_specs=(
            P("blk", None, "tp"),
            P("blk", None, "tp"),
            P("blk", None, "tp"),
            P("blk", None, "tp"),
            P("tp", None),
            P("blk"),
            P("blk", None),
            P("blk"),
            P("blk"),
        ),
        out_specs=P("blk", None, "tp"),
        check_vma=False,
    )
```
